32 devices in a mesh: grp: 4 (over z), sub: 4 (over y, x), rep: 2 (over core).
Axes of the slice: x: 2, y: 2, z: 4, core: 2. Of those that a mesh axis runs over, the one named last changes fastest.
Arguments:
- starting_concentration_per_run: float32 [4, 8, 256, 512], P('grp', None, 'sub', 'rep'), may hold values from -6 to 6
- diffusivity: float32 [256, 512], P('sub', 'rep'), may hold values from 0.02 to 0.12
- run_layer_stability_number: float32 [4, 8], P('grp'), may hold values from 0.05 to 0.4
- observed: float32 [256, 4, 128], P(('sub', 'grp'), 'rep'), may hold values from -6 to 6
- slot_error_variance: float32 [256, 4, 128], P(('sub', 'grp'), 'rep'), may hold values from 0.25 to 4
- sensor_target_site: int32 [256, 4, 128], P(('sub', 'grp'), 'rep'), may hold values from 0 to 1023
- patch_live_count: int32 [256, 4], P(('sub', 'grp'), 'rep'), may hold values from 1 to 128, as said below
Outputs:
- analysis: float32 [4, 8, 256, 512], P('grp', None, 'sub', 'rep')
The draws below stay inside these ranges and needn't reach their ends.
Inputs may be any that keep to these rules, and one draw needn't show every extreme that they name: Slots below patch_live_count of a patch are live, the rest are unused; some patch has all 128 slots live. `sensor_target_site`: A slot observes the cell level * 128 + column of its own patch.
All inputs are finite; a program needn't handle non-finite values.
Results may differ from the reference program's by a relative error of at most 0.0003.
Values sent between devices are 32-bit elements; how exact they have to be, the bound alone decides.
A program may use at most 64 MiB of HBM per device.

```python
import math
import jax
import jax.numpy as jnp
from jax import lax

VERTICAL_LEVELS = 8
PATCH = 128
SLOTS = 128
STEPS = 4
NS_ITERS = 4
ENSEMBLE_SIZE = 4
GRID_ROWS = 256
GRID_COLUMNS = 512
NXP = 4


def draw_patch_live_count(key, part):
    first_key, second_key = jax.random.split(jax.random.fold_in(key, 11))
    uniform_int = jax.random.randint(first_key, (GRID_ROWS * NXP,), 0, 1024)
    cubed = uniform_int * uniform_int // 1024 * uniform_int // 1024
    counts = 1 + cubed * (SLOTS - 1) // 1023
    position = jax.random.randint(second_key, (), 0, GRID_ROWS * NXP)
    counts = counts.at[position].set(SLOTS)
    return counts.reshape(GRID_ROWS, NXP).astype(jnp.int32)


def with_ends(array, key, low, high):
    extent = array.shape
    place = [jax.random.randint(jax.random.fold_in(key, axis), (), 0, extent[axis]) for axis in range(len(extent))]
    array = array.at[tuple(place)].set(low)
    longest = extent.index(max(extent))
    place[longest] = (place[longest] + 1) % extent[longest]
    return array.at[tuple(place)].set(high)


def shard_levels(own_key, extent, cuts, low, high):
    loudness = 1.0
    for dim, shards_of in cuts:
        draws = jax.random.uniform(jax.random.fold_in(jax.random.fold_in(own_key, 6), dim), (shards_of,), jnp.float32, low / len(cuts), high / len(cuts))
        loudness = loudness * jnp.repeat(jnp.exp(draws), extent[dim] // shards_of).reshape((-1,) + (1,) * (len(extent) - 1 - dim))
    return loudness


def centred(stream_key, shape, width, most, cuts=(), kind=jnp.bfloat16):
    drawn = width * jax.random.normal(stream_key, shape, jnp.float32)
    if cuts:
        drawn = drawn * shard_levels(stream_key, shape, cuts, -0.22, 0.18)
    return jnp.clip(drawn, -most, most).astype(kind)


def setup_inputs(seed: int = 0) -> dict:
    keys = jax.random.split(jax.random.key(seed), 8)
    starting_concentration_per_run = centred(keys[0], (ENSEMBLE_SIZE, VERTICAL_LEVELS, GRID_ROWS, GRID_COLUMNS), 1.0, 6.0, ((0, 4), (2, 4), (3, 2)), jnp.float32)
    diffusivity = jnp.clip(jnp.exp(math.log(0.12) - 1.7917595 * jax.random.uniform(keys[1], (GRID_ROWS, GRID_COLUMNS), jnp.float32) ** shard_levels(keys[1], (GRID_ROWS, GRID_COLUMNS), ((0, 4), (1, 2)), -0.2, 0.2)), 0.02, 0.12)
    run_layer_stability_number = jnp.clip(jnp.exp(math.log(0.4) - 2.0794415 * jax.random.uniform(keys[2], (ENSEMBLE_SIZE, VERTICAL_LEVELS), jnp.float32) ** shard_levels(keys[2], (ENSEMBLE_SIZE, VERTICAL_LEVELS), ((0, 4),), -0.2, 0.2)), 0.05, 0.4)
    observed = centred(keys[3], (GRID_ROWS, NXP, SLOTS), 1.0, 6.0, ((0, 16), (1, 2)), jnp.float32)
    slot_error_variance = jnp.clip(jnp.exp(math.log(4.0) - 2.7725887 * jax.random.uniform(keys[4], (GRID_ROWS, NXP, SLOTS), jnp.float32) ** shard_levels(keys[4], (GRID_ROWS, NXP, SLOTS), ((0, 16), (1, 2)), -0.2, 0.2)), 0.25, 4.0)
    sensor_target_site = with_ends(jax.random.randint(keys[5], (GRID_ROWS, NXP, SLOTS), 0, VERTICAL_LEVELS * PATCH), jax.random.fold_in(keys[5], 1), 0, (VERTICAL_LEVELS * PATCH) - 1).astype(jnp.int32)
    patch_live_count = draw_patch_live_count(jax.random.fold_in(keys[7], 71), 0)
    return dict(starting_concentration_per_run=starting_concentration_per_run, diffusivity=diffusivity, run_layer_stability_number=run_layer_stability_number, observed=observed, slot_error_variance=slot_error_variance, sensor_target_site=sensor_target_site, patch_live_count=patch_live_count)


HIGHEST = lax.Precision.HIGHEST

def advance(padded, diffusivity, member_wind):
    centre = padded[..., 1:-1, 1:-1]
    northern = padded[..., :-2, 1:-1]
    southern = padded[..., 2:, 1:-1]
    western = padded[..., 1:-1, :-2]
    easterly_side = padded[..., 1:-1, 2:]
    spread = northern + southern + (western + easterly_side) - 4.0 * centre
    return centre + diffusivity * spread - member_wind * (centre - western)

def analyse(background, sampled, observed, slot_error_variance, patch_live_count):
    members = background.shape[1]
    slots = observed.shape[-1]
    centre_mean = lax.optimization_barrier(jnp.mean(background, axis=1, keepdims=True))
    perturbed = background - centre_mean
    sampled_mean = lax.optimization_barrier(jnp.mean(sampled, axis=1, keepdims=True))
    sampled_pert = sampled - sampled_mean
    live_slot = jnp.arange(slots)[None, :] < patch_live_count[:, None]
    precision_obs = jnp.where(live_slot, 1.0 / slot_error_variance, 0.0 * slot_error_variance)
    innovation = observed - sampled_mean[:, 0, :]
    weighted = sampled_pert * precision_obs[:, None, :]
    identity = jnp.eye(members, dtype=background.dtype)
    system = jnp.einsum('pms,pns->pmn', weighted, sampled_pert, precision=HIGHEST) + (members - 1.0) * identity
    source_term = jnp.einsum('pms,ps->pm', weighted, innovation, precision=HIGHEST)
    factor = jnp.linalg.cholesky(system)
    halfway = lax.linalg.triangular_solve(factor, source_term[:, :, None], left_side=True, lower=True)
    mean_weight = lax.linalg.triangular_solve(factor, halfway, left_side=True, lower=True, transpose_a=True)[:, :, 0]
    norm_scale = jnp.sqrt(lax.optimization_barrier(jnp.sum(system * system, axis=(1, 2))))
    iterate = system / norm_scale[:, None, None]
    inverse_root = jnp.broadcast_to(identity, system.shape)
    for sweep in range(NS_ITERS):
        update = 1.5 * identity - 0.5 * jnp.einsum('pij,pjk->pik', inverse_root, iterate, precision=HIGHEST)
        iterate = jnp.einsum('pij,pjk->pik', iterate, update, precision=HIGHEST)
        inverse_root = jnp.einsum('pij,pjk->pik', update, inverse_root, precision=HIGHEST)
    spread_weight = inverse_root * jnp.sqrt((members - 1.0) / norm_scale)[:, None, None]
    combined = spread_weight + mean_weight[:, :, None]
    return centre_mean + jnp.einsum('pki,pkc->pic', combined, perturbed, precision=HIGHEST)

def reference(starting_concentration_per_run, diffusivity, run_layer_stability_number, observed, slot_error_variance, sensor_target_site, patch_live_count):

    def march_single_run(inputs):
        member_state, member_wind = inputs
        for stepno in range(STEPS):
            padded = jnp.pad(member_state, ((0, 0), (1, 1), (1, 1)))
            member_state = advance(padded, diffusivity, member_wind[:, None, None])
        return member_state
    predicted_concentration = lax.map(march_single_run, (starting_concentration_per_run, run_layer_stability_number))
    line_by_line = jnp.transpose(predicted_concentration, (2, 0, 1, 3))

    def analyse_row(inputs):
        row_state, row_observed, row_variance, row_cell, row_count = inputs
        members, levels, row_width = row_state.shape
        patches = row_width // PATCH
        background = jnp.transpose(row_state.reshape(members, levels, patches, PATCH), (2, 0, 1, 3)).reshape(patches, members, levels * PATCH)
        cell_index = jnp.broadcast_to(row_cell[:, None, :], (patches, members, row_cell.shape[-1]))
        sampled = jnp.take_along_axis(background, cell_index, axis=2)
        result = analyse(background, sampled, row_observed, row_variance, row_count)
        return jnp.transpose(result.reshape(patches, members, levels, PATCH), (1, 2, 0, 3)).reshape(members, levels, row_width)
    analysed = lax.map(analyse_row, (line_by_line, observed, slot_error_variance, sensor_target_site, patch_live_count))
    return jnp.transpose(analysed, (1, 2, 0, 3))
```

```python
import functools

import jax
import jax.numpy as jnp
from jax import lax
from jax.experimental import pallas as pl
from jax.experimental.pallas import tpu as pltpu
from jax.sharding import PartitionSpec as P

PATCH = 128
STEPS = 4
NS_ITERS = 4


HIGHEST = lax.Precision.HIGHEST


def extended(x, sides, width):
    for axis, dim in sides:
        devices, length = (lax.axis_size(axis), x.shape[dim])
        up = [(i, (i + 1) % devices) for i in range(devices - 1)]
        down = [(j, i) for i, j in up]
        last = lax.slice_in_dim(x, length - width, length, axis=dim)
        initial = lax.slice_in_dim(x, 0, width, axis=dim)
        before = lax.ppermute(last, axis, up)
        after = lax.ppermute(initial, axis, down)
        x = jnp.concatenate([before, x, after], axis=dim)
    return x


def advance(padded, diffusivity, member_wind):
    centre = padded[..., 1:-1, 1:-1]
    northern = padded[..., :-2, 1:-1]
    southern = padded[..., 2:, 1:-1]
    western = padded[..., 1:-1, :-2]
    easterly_side = padded[..., 1:-1, 2:]
    spread = northern + southern + (western + easterly_side) - 4.0 * centre
    return centre + diffusivity * spread - member_wind * (centre - western)


def analyse(background, sampled, observed, slot_error_variance, patch_live_count):
    members = background.shape[1]
    slots = observed.shape[-1]
    centre_mean = jnp.mean(background, axis=1, keepdims=True)
    perturbed = background - centre_mean
    sampled_mean = jnp.mean(sampled, axis=1, keepdims=True)
    sampled_pert = sampled - sampled_mean
    live_slot = jnp.arange(slots)[None, :] < patch_live_count[:, None]
    precision_obs = jnp.where(live_slot, 1.0 / slot_error_variance, 0.0 * slot_error_variance)
    innovation = observed - sampled_mean[:, 0, :]
    weighted = sampled_pert * precision_obs[:, None, :]
    identity = jnp.eye(members, dtype=background.dtype)
    system = (
        jnp.einsum("pms,pns->pmn", weighted, sampled_pert, precision=HIGHEST)
        + (members - 1.0) * identity
    )
    source_term = jnp.einsum("pms,ps->pm", weighted, innovation, precision=HIGHEST)
    factor = jnp.linalg.cholesky(system)
    halfway = lax.linalg.triangular_solve(
        factor, source_term[:, :, None], left_side=True, lower=True
    )
    mean_weight = lax.linalg.triangular_solve(
        factor, halfway, left_side=True, lower=True, transpose_a=True
    )[:, :, 0]
    norm_scale = jnp.sqrt(jnp.sum(system * system, axis=(1, 2)))
    iterate = system / norm_scale[:, None, None]
    inverse_root = jnp.broadcast_to(identity, system.shape)
    for sweep in range(NS_ITERS):
        update = 1.5 * identity - 0.5 * jnp.einsum(
            "pij,pjk->pik", inverse_root, iterate, precision=HIGHEST
        )
        iterate = jnp.einsum("pij,pjk->pik", iterate, update, precision=HIGHEST)
        inverse_root = jnp.einsum("pij,pjk->pik", update, inverse_root, precision=HIGHEST)
    spread_weight = inverse_root * jnp.sqrt((members - 1.0) / norm_scale)[:, None, None]
    combined = spread_weight + mean_weight[:, :, None]
    return centre_mean + jnp.einsum("pki,pkc->pic", combined, perturbed, precision=HIGHEST)


def on_device_plain(
    starting_concentration_per_run,
    diffusivity,
    run_layer_stability_number,
    observed,
    slot_error_variance,
    sensor_target_site,
    patch_live_count,
):
    member_wind = run_layer_stability_number[:, :, None, None]
    present_state = starting_concentration_per_run
    for stepno in range(STEPS):
        padded = extended(present_state, (("sub", 2), ("rep", 3)), 1)
        present_state = advance(padded, diffusivity, member_wind)
    gathered = lax.all_to_all(present_state, "grp", split_axis=2, concat_axis=0, tiled=True)
    members, levels, row_group, row_width = gathered.shape
    patches = row_width // PATCH
    background = jnp.transpose(
        gathered.reshape(members, levels, row_group, patches, PATCH), (2, 3, 0, 1, 4)
    ).reshape(row_group * patches, members, levels * PATCH)
    slots = observed.shape[-1]
    cell_flat = sensor_target_site.reshape(-1, slots)
    selector = (cell_flat[:, :, None] == jnp.arange(levels * PATCH)[None, None, :]).astype(
        jnp.float32
    )
    sampled = jnp.einsum("pmc,psc->pms", background, selector, precision=HIGHEST)
    result = analyse(
        background,
        sampled,
        observed.reshape(-1, slots),
        slot_error_variance.reshape(-1, slots),
        patch_live_count.reshape(-1),
    )
    returned = jnp.transpose(
        result.reshape(row_group, patches, members, levels, PATCH), (2, 3, 0, 1, 4)
    ).reshape(members, levels, row_group, row_width)
    return lax.all_to_all(returned, "grp", split_axis=0, concat_axis=2, tiled=True)


EDGE = 8
LANES = 128
MESH = pl.DeviceIdType.MESH


def sym_product(a, b):
    size = len(a)
    c = [[None] * size for _ in range(size)]
    for i in range(size):
        for j in range(i, size):
            total = a[i][0] * b[0][j]
            for k in range(1, size):
                total = total + a[i][k] * b[k][j]
            c[i][j] = c[j][i] = total
    return c


def weights(system, source):
    size = len(system)
    low = [[None] * size for _ in range(size)]
    for j in range(size):
        diag = system[j][j]
        for k in range(j):
            diag = diag - low[j][k] * low[j][k]
        low[j][j] = jnp.sqrt(diag)
        for i in range(j + 1, size):
            v = system[i][j]
            for k in range(j):
                v = v - low[i][k] * low[j][k]
            low[i][j] = v / low[j][j]
    half = []
    for i in range(size):
        v = source[i]
        for k in range(i):
            v = v - low[i][k] * half[k]
        half.append(v / low[i][i])
    mean_weight = [None] * size
    for i in reversed(range(size)):
        v = half[i]
        for k in range(i + 1, size):
            v = v - low[k][i] * mean_weight[k]
        mean_weight[i] = v / low[i][i]
    total = None
    for i in range(size):
        for j in range(size):
            sq = system[i][j] * system[i][j]
            total = sq if total is None else total + sq
    norm_scale = jnp.sqrt(total)
    iterate = [[None] * size for _ in range(size)]
    for i in range(size):
        for j in range(i, size):
            iterate[i][j] = iterate[j][i] = system[i][j] / norm_scale
    root = None
    for sweep in range(NS_ITERS):
        prod = iterate if root is None else sym_product(root, iterate)
        update = [[None] * size for _ in range(size)]
        for i in range(size):
            for j in range(i, size):
                v = -0.5 * prod[i][j]
                update[i][j] = update[j][i] = 1.5 + v if i == j else v
        if sweep < NS_ITERS - 1:
            iterate = sym_product(iterate, update)
        root = update if root is None else sym_product(update, root)
    scale = jnp.sqrt((size - 1.0) / norm_scale)
    return [[root[k][i] * scale + mean_weight[k] for i in range(size)] for k in range(size)]


def kernel(
    sizes, x_ref, d_ref, wind, obs, var, site, count, out,
    field, inside, made, ground, result, up_send, down_send, up_recv, down_recv,
    cols_send, cols_recv, load_sem, halo_send, halo_recv, ens_send, ens_recv, back_send, back_recv, own_sem,
):
    groups, subs, levels, high, wide, band, patches = sizes
    me, mine, core = lax.axis_index("grp"), lax.axis_index("sub"), lax.axis_index("rep")
    other = 1 - core
    tall, across = high + 2 * EDGE, wide + LANES
    has_up, has_down = mine > 0, mine < subs - 1
    loads = [
        pltpu.make_async_copy(x_ref, field.at[pl.ds(0, levels), pl.ds(EDGE, high), pl.ds(0, wide)], load_sem.at[0]),
        pltpu.make_async_copy(d_ref, field.at[levels, pl.ds(EDGE, high), pl.ds(0, wide)], load_sem.at[1]),
    ]
    for c in loads:
        c.start()

    barrier = pltpu.get_barrier_semaphore()
    for step in range(1, groups):
        peer = lax.rem(me + step, groups)
        pl.semaphore_signal(barrier, inc=1, device_id={"grp": peer}, device_id_type=MESH)
    pl.semaphore_signal(barrier, inc=1, device_id={"rep": other}, device_id_type=MESH)

    @pl.when(has_up)
    def _():
        pl.semaphore_signal(barrier, inc=1, device_id={"sub": mine - 1}, device_id_type=MESH)
        pl.semaphore_signal(barrier, inc=1, device_id={"sub": mine - 1, "rep": other}, device_id_type=MESH)

    @pl.when(has_down)
    def _():
        pl.semaphore_signal(barrier, inc=1, device_id={"sub": mine + 1}, device_id_type=MESH)
        pl.semaphore_signal(barrier, inc=1, device_id={"sub": mine + 1, "rep": other}, device_id_type=MESH)

    row = lax.broadcasted_iota(jnp.int32, (tall, across), 0) - EDGE
    col = lax.broadcasted_iota(jnp.int32, (tall, across), 1)
    row_ok = ((row >= 0) | has_up) & ((row < high) | has_down)
    row_ok = row_ok & (row >= -STEPS) & (row < high + STEPS)
    col_ok = (col < wide) | ((col < wide + STEPS) & (core == 0)) | ((col >= across - STEPS) & (core > 0))
    inside[...] = jnp.where(row_ok & col_ok, 1.0, 0.0)

    for c in loads:
        c.wait()

    fields = levels + 1
    lane = lax.broadcasted_iota(jnp.int32, (high, LANES), 1)
    slot_of_lane = lax.rem(lane + STEPS, LANES) // (2 * STEPS)
    packed = jnp.zeros((high, LANES), jnp.float32)
    for f in range(fields):
        inner = field[f, EDGE : EDGE + high, wide - LANES : wide]
        outer = field[f, EDGE : EDGE + high, 0:LANES]
        tile = jnp.where(core == 0, inner, outer)
        if f:
            tile = pltpu.roll(tile, 2 * STEPS * f, 1)
        packed = jnp.where(slot_of_lane == f, tile, packed)
    cols_send[...] = packed
    sub_row = lax.broadcasted_iota(jnp.int32, (EDGE, wide), 0)
    for k in range((fields + 1) // 2):
        a, b = 2 * k, min(2 * k + 1, fields - 1)
        top_a, top_b = field[a, EDGE : 2 * EDGE, 0:wide], field[b, EDGE : 2 * EDGE, 0:wide]
        low_a, low_b = field[a, high : high + EDGE, 0:wide], field[b, high : high + EDGE, 0:wide]
        up_send[k] = jnp.where(sub_row < STEPS, top_a, pltpu.roll(top_b, STEPS, 0))
        down_send[k] = jnp.where(sub_row >= STEPS, low_a, pltpu.roll(low_b, STEPS, 0))

    pl.semaphore_wait(
        barrier, groups + 2 * has_up.astype(jnp.int32) + 2 * has_down.astype(jnp.int32)
    )

    def halo(src, dst, n, device):
        return pltpu.make_async_remote_copy(
            src_ref=src, dst_ref=dst, send_sem=halo_send.at[n], recv_sem=halo_recv.at[n],
            device_id=device, device_id_type=MESH,
        )

    beside = halo(cols_send, cols_recv.at[pl.ds(EDGE, high)], 0, {"rep": other})
    beside.start()
    upward = [
        halo(up_send, down_recv, 1, {"sub": mine - 1}),
        halo(cols_send.at[pl.ds(0, EDGE)], cols_recv.at[pl.ds(EDGE + high, EDGE)], 2, {"sub": mine - 1, "rep": other}),
    ]
    downward = [
        halo(down_send, up_recv, 3, {"sub": mine + 1}),
        halo(cols_send.at[pl.ds(high - EDGE, EDGE)], cols_recv.at[pl.ds(0, EDGE)], 4, {"sub": mine + 1, "rep": other}),
    ]

    @pl.when(has_up)
    def _():
        for c in upward:
            c.start()

    @pl.when(has_down)
    def _():
        for c in downward:
            c.start()

    beside.wait_recv()

    def place_columns(first, rows):
        got = cols_recv[first : first + rows]
        ok = inside[first : first + rows, wide:across] > 0.0
        for f in range(fields):
            tile = pltpu.roll(got, LANES - 2 * STEPS * f, 1) if f else got
            field[f, first : first + rows, wide:across] = jnp.where(ok, tile, 0.0)

    place_columns(EDGE, high)

    def forecast(level, first, rows):
        q = field[level, first : first + rows]
        d = field[levels, first : first + rows]
        wind_here = inside[first : first + rows] * wind[0, level]
        for _ in range(STEPS):
            west = pltpu.roll(q, 1, 1)
            east = pltpu.roll(q, across - 1, 1)
            north = pltpu.roll(q, 1, 0)
            south = pltpu.roll(q, rows - 1, 0)
            spread = (north + south) + (west + east) - 4.0 * q
            q = q + d * spread - wind_here * (q - west)
        return q[EDGE : rows - EDGE, 0:wide]

    def ensemble(level, target, owner):
        return pltpu.make_async_remote_copy(
            src_ref=made.at[level, pl.ds(target * band, band)],
            dst_ref=ground.at[owner, level],
            send_sem=ens_send.at[target], recv_sem=ens_recv.at[owner],
            device_id={"grp": target}, device_id_type=MESH,
        )

    def send_band(level, target):
        @pl.when(me != target)
        def _():
            ensemble(level, target, me).start()

    def middle(level, carry):
        made[level, band : high - band] = forecast(level, band, high - 2 * band + 2 * EDGE)
        for target in range(1, groups - 1):
            send_band(level, target)
        return carry

    lax.fori_loop(0, levels, middle, 0)

    @pl.when(has_up)
    def _():
        for c in downward:
            c.wait_recv()

    @pl.when(has_down)
    def _():
        for c in upward:
            c.wait_recv()

    place_columns(0, EDGE)
    place_columns(EDGE + high, EDGE)
    for f in range(fields):
        above, below = up_recv[f // 2], down_recv[f // 2]
        if f % 2:
            above, below = pltpu.roll(above, STEPS, 0), pltpu.roll(below, STEPS, 0)
        field[f, 0:EDGE, 0:wide] = jnp.where(inside[0:EDGE, 0:wide] > 0.0, above, 0.0)
        field[f, EDGE + high : tall, 0:wide] = jnp.where(inside[EDGE + high : tall, 0:wide] > 0.0, below, 0.0)

    def outer_bands(level, carry):
        made[level, 0:band] = forecast(level, 0, band + 2 * EDGE)
        send_band(level, 0)
        made[level, high - band : high] = forecast(level, high - band, band + 2 * EDGE)
        send_band(level, groups - 1)
        return carry

    lax.fori_loop(0, levels, outer_bands, 0)
    ground[me] = made[:, pl.ds(pl.multiple_of(me * band, band), band), :]

    def whole_band(target, owner):
        return pltpu.make_async_remote_copy(
            src_ref=made.at[:, pl.ds(target * band, band)],
            dst_ref=ground.at[owner],
            send_sem=ens_send.at[target], recv_sem=ens_recv.at[owner],
            device_id={"grp": target}, device_id_type=MESH,
        )

    for step in range(1, groups):
        peer = lax.rem(me + step, groups)
        whole_band(peer, peer).wait_recv()

    patch = wide // patches
    tiles = [(h, p) for h in range(band // EDGE) for p in range(patches)]
    shape = (EDGE, LANES)
    lanes = lax.broadcasted_iota(jnp.int32, shape, 1)
    system = [[None] * groups for _ in range(groups)]
    source = [None] * groups

    def put(old, new, index):
        new = jnp.broadcast_to(new, shape)
        return new if old is None else jnp.where(lanes == index, new, old)

    for index, (h, p) in enumerate(tiles):
        rows = slice(h * EDGE, (h + 1) * EDGE)
        here = site[rows, p, :]
        level_of, col_of = here // patch, lax.rem(here, patch)
        sampled = []
        for m in range(groups):
            got = jnp.zeros(shape, jnp.float32)
            for l in range(levels):
                tile = ground[m, l, rows, p * patch : (p + 1) * patch]
                pick = jnp.take_along_axis(tile, col_of, axis=1, mode="promise_in_bounds")
                got = jnp.where(level_of == l, pick, got)
            sampled.append(got)
        mean = sum(sampled[1:], sampled[0]) * (1.0 / groups)
        pert = [s - mean for s in sampled]
        precision = jnp.where(lanes < count[rows, p : p + 1], 1.0 / var[rows, p, :], 0.0)
        innovation = obs[rows, p, :] - mean
        for i in range(groups):
            weighted = pert[i] * precision
            source[i] = put(source[i], jnp.sum(weighted * innovation, axis=1, keepdims=True), index)
            for j in range(i, groups):
                v = jnp.sum(weighted * pert[j], axis=1, keepdims=True)
                v = v + (groups - 1.0) if i == j else v
                system[i][j] = system[j][i] = put(system[i][j], v, index)
    combined = weights(system, source)

    def back(h, target, owner):
        return pltpu.make_async_remote_copy(
            src_ref=result.at[target, :, pl.ds(h * EDGE, EDGE)],
            dst_ref=out.at[:, pl.ds(owner * band + h * EDGE, EDGE)],
            send_sem=back_send.at[target], recv_sem=back_recv.at[owner],
            device_id={"grp": target}, device_id_type=MESH,
        )

    for h in range(band // EDGE):
        rows = slice(h * EDGE, (h + 1) * EDGE)
        for p in range(patches):
            index = h * patches + p
            c = [
                [jnp.broadcast_to(combined[k][i][:, index : index + 1], shape) for i in range(groups)]
                for k in range(groups)
            ]
            cells = slice(p * patch, (p + 1) * patch)
            for l in range(levels):
                member = [ground[m, l, rows, cells] for m in range(groups)]
                mean = sum(member[1:], member[0]) * (1.0 / groups)
                pert = [v - mean for v in member]
                for i in range(groups):
                    v = c[0][i] * pert[0]
                    for k in range(1, groups):
                        v = v + c[k][i] * pert[k]
                    result[i, l, rows, cells] = mean + v
        for step in range(1, groups):
            peer = lax.rem(me + step, groups)
            back(h, peer, me).start()
    own = pltpu.make_async_copy(result.at[me], out.at[:, pl.ds(me * band, band)], own_sem)
    own.start()

    beside.wait_send()

    @pl.when(has_up)
    def _():
        for c in upward:
            c.wait_send()

    @pl.when(has_down)
    def _():
        for c in downward:
            c.wait_send()

    def whole_back(target, owner):
        return pltpu.make_async_remote_copy(
            src_ref=result.at[target],
            dst_ref=out.at[:, pl.ds(owner * band, band)],
            send_sem=back_send.at[target], recv_sem=back_recv.at[owner],
            device_id={"grp": target}, device_id_type=MESH,
        )

    for step in range(1, groups):
        peer = lax.rem(me + step, groups)
        whole_band(peer, me).wait_send()
        whole_back(peer, me).wait_send()
        whole_back(peer, peer).wait_recv()
    own.wait()


def fused(state, diffusivity, wind, observed, variance, site, count):
    groups, subs = lax.axis_size("grp"), lax.axis_size("sub")
    _, levels, high, wide = state.shape
    band, patches, _ = observed.shape
    tall, across = high + 2 * EDGE, wide + LANES
    pairs = (levels + 2) // 2
    f32 = jnp.float32
    vmem, dma = pltpu.VMEM, pltpu.SemaphoreType.DMA
    whole = pl.BlockSpec(memory_space=pltpu.VMEM)
    anywhere = pl.BlockSpec(memory_space=pl.ANY)
    sizes = (groups, subs, levels, high, wide, band, patches)
    out = pl.pallas_call(
        functools.partial(kernel, sizes),
        out_shape=jax.ShapeDtypeStruct((levels, high, wide), f32),
        in_specs=[anywhere, anywhere, pl.BlockSpec(memory_space=pltpu.SMEM), whole, whole, whole, whole],
        out_specs=anywhere,
        scratch_shapes=[
            vmem((levels + 1, tall, across), f32),
            vmem((tall, across), f32),
            vmem((levels, high, wide), f32),
            vmem((groups, levels, band, wide), f32),
            vmem((groups, levels, band, wide), f32),
            vmem((pairs, EDGE, wide), f32),
            vmem((pairs, EDGE, wide), f32),
            vmem((pairs, EDGE, wide), f32),
            vmem((pairs, EDGE, wide), f32),
            vmem((high, LANES), f32),
            vmem((tall, LANES), f32),
            dma((2,)),
            dma((5,)),
            dma((5,)),
            dma((groups,)),
            dma((groups,)),
            dma((groups,)),
            dma((groups,)),
            dma(()),
        ],
        compiler_params=pltpu.CompilerParams(collective_id=0, has_side_effects=True),
    )(state[0], diffusivity, wind, observed, variance, site, count)
    return out[None]


def on_device(
    starting_concentration_per_run,
    diffusivity,
    run_layer_stability_number,
    observed,
    slot_error_variance,
    sensor_target_site,
    patch_live_count,
):
    groups, subs, reps = lax.axis_size("grp"), lax.axis_size("sub"), lax.axis_size("rep")
    members, levels, high, wide = starting_concentration_per_run.shape
    band, patches, slots = observed.shape
    fits = (
        members == 1
        and reps == 2
        and 3 <= groups <= 8
        and subs >= 2
        and band % EDGE == 0
        and 2 * STEPS * (levels + 1) <= LANES
        and wide == patches * PATCH
        and PATCH == LANES == slots
    )
    step = fused if fits else on_device_plain
    return step(
        starting_concentration_per_run,
        diffusivity,
        run_layer_stability_number,
        observed,
        slot_error_variance,
        sensor_target_site,
        patch_live_count,
    )


def solution(mesh):
    in_specs = (
        P("grp", None, "sub", "rep"),
        P("sub", "rep"),
        P("grp", None),
        P(("sub", "grp"), "rep", None),
        P(("sub", "grp"), "rep", None),
        P(("sub", "grp"), "rep", None),
        P(("sub", "grp"), "rep"),
    )
    out_specs = P("grp", None, "sub", "rep")
    return jax.shard_map(
        on_device, mesh=mesh, in_specs=in_specs, out_specs=out_specs, check_vma=False
    )
```

```python
import functools

import jax
import jax.numpy as jnp
from jax import lax
from jax.experimental import pallas as pl
from jax.experimental.pallas import tpu as pltpu
from jax.sharding import PartitionSpec as P

PATCH = 128
STEPS = 4
NS_ITERS = 4


HIGHEST = lax.Precision.HIGHEST


def extended(x, sides, width):
    for axis, dim in sides:
        devices, length = (lax.axis_size(axis), x.shape[dim])
        up = [(i, (i + 1) % devices) for i in range(devices - 1)]
        down = [(j, i) for i, j in up]
        last = lax.slice_in_dim(x, length - width, length, axis=dim)
        initial = lax.slice_in_dim(x, 0, width, axis=dim)
        before = lax.ppermute(last, axis, up)
        after = lax.ppermute(initial, axis, down)
        x = jnp.concatenate([before, x, after], axis=dim)
    return x


def advance(padded, diffusivity, member_wind):
    centre = padded[..., 1:-1, 1:-1]
    northern = padded[..., :-2, 1:-1]
    southern = padded[..., 2:, 1:-1]
    western = padded[..., 1:-1, :-2]
    easterly_side = padded[..., 1:-1, 2:]
    spread = northern + southern + (western + easterly_side) - 4.0 * centre
    return centre + diffusivity * spread - member_wind * (centre - western)


def analyse(background, sampled, observed, slot_error_variance, patch_live_count):
    members = background.shape[1]
    slots = observed.shape[-1]
    centre_mean = jnp.mean(background, axis=1, keepdims=True)
    perturbed = background - centre_mean
    sampled_mean = jnp.mean(sampled, axis=1, keepdims=True)
    sampled_pert = sampled - sampled_mean
    live_slot = jnp.arange(slots)[None, :] < patch_live_count[:, None]
    precision_obs = jnp.where(live_slot, 1.0 / slot_error_variance, 0.0 * slot_error_variance)
    innovation = observed - sampled_mean[:, 0, :]
    weighted = sampled_pert * precision_obs[:, None, :]
    identity = jnp.eye(members, dtype=background.dtype)
    system = (
        jnp.einsum("pms,pns->pmn", weighted, sampled_pert, precision=HIGHEST)
        + (members - 1.0) * identity
    )
    source_term = jnp.einsum("pms,ps->pm", weighted, innovation, precision=HIGHEST)
    factor = jnp.linalg.cholesky(system)
    halfway = lax.linalg.triangular_solve(
        factor, source_term[:, :, None], left_side=True, lower=True
    )
    mean_weight = lax.linalg.triangular_solve(
        factor, halfway, left_side=True, lower=True, transpose_a=True
    )[:, :, 0]
    norm_scale = jnp.sqrt(jnp.sum(system * system, axis=(1, 2)))
    iterate = system / norm_scale[:, None, None]
    inverse_root = jnp.broadcast_to(identity, system.shape)
    for sweep in range(NS_ITERS):
        update = 1.5 * identity - 0.5 * jnp.einsum(
            "pij,pjk->pik", inverse_root, iterate, precision=HIGHEST
        )
        iterate = jnp.einsum("pij,pjk->pik", iterate, update, precision=HIGHEST)
        inverse_root = jnp.einsum("pij,pjk->pik", update, inverse_root, precision=HIGHEST)
    spread_weight = inverse_root * jnp.sqrt((members - 1.0) / norm_scale)[:, None, None]
    combined = spread_weight + mean_weight[:, :, None]
    return centre_mean + jnp.einsum("pki,pkc->pic", combined, perturbed, precision=HIGHEST)


def on_device_plain(
    starting_concentration_per_run,
    diffusivity,
    run_layer_stability_number,
    observed,
    slot_error_variance,
    sensor_target_site,
    patch_live_count,
):
    member_wind = run_layer_stability_number[:, :, None, None]
    present_state = starting_concentration_per_run
    for stepno in range(STEPS):
        padded = extended(present_state, (("sub", 2), ("rep", 3)), 1)
        present_state = advance(padded, diffusivity, member_wind)
    gathered = lax.all_to_all(present_state, "grp", split_axis=2, concat_axis=0, tiled=True)
    members, levels, row_group, row_width = gathered.shape
    patches = row_width // PATCH
    background = jnp.transpose(
        gathered.reshape(members, levels, row_group, patches, PATCH), (2, 3, 0, 1, 4)
    ).reshape(row_group * patches, members, levels * PATCH)
    slots = observed.shape[-1]
    cell_flat = sensor_target_site.reshape(-1, slots)
    selector = (cell_flat[:, :, None] == jnp.arange(levels * PATCH)[None, None, :]).astype(
        jnp.float32
    )
    sampled = jnp.einsum("pmc,psc->pms", background, selector, precision=HIGHEST)
    result = analyse(
        background,
        sampled,
        observed.reshape(-1, slots),
        slot_error_variance.reshape(-1, slots),
        patch_live_count.reshape(-1),
    )
    returned = jnp.transpose(
        result.reshape(row_group, patches, members, levels, PATCH), (2, 3, 0, 1, 4)
    ).reshape(members, levels, row_group, row_width)
    return lax.all_to_all(returned, "grp", split_axis=0, concat_axis=2, tiled=True)


EDGE = 8
SCOPED = 24 * 1024 * 1024
LANES = 128
MESH = pl.DeviceIdType.MESH


def sym_product(a, b):
    size = len(a)
    c = [[None] * size for _ in range(size)]
    for i in range(size):
        for j in range(i, size):
            total = a[i][0] * b[0][j]
            for k in range(1, size):
                total = total + a[i][k] * b[k][j]
            c[i][j] = c[j][i] = total
    return c


def weights(system, source):
    size = len(system)
    low = [[None] * size for _ in range(size)]
    for j in range(size):
        diag = system[j][j]
        for k in range(j):
            diag = diag - low[j][k] * low[j][k]
        low[j][j] = jnp.sqrt(diag)
        for i in range(j + 1, size):
            v = system[i][j]
            for k in range(j):
                v = v - low[i][k] * low[j][k]
            low[i][j] = v / low[j][j]
    half = []
    for i in range(size):
        v = source[i]
        for k in range(i):
            v = v - low[i][k] * half[k]
        half.append(v / low[i][i])
    mean_weight = [None] * size
    for i in reversed(range(size)):
        v = half[i]
        for k in range(i + 1, size):
            v = v - low[k][i] * mean_weight[k]
        mean_weight[i] = v / low[i][i]
    total = None
    for i in range(size):
        for j in range(size):
            sq = system[i][j] * system[i][j]
            total = sq if total is None else total + sq
    norm_scale = jnp.sqrt(total)
    iterate = [[None] * size for _ in range(size)]
    for i in range(size):
        for j in range(i, size):
            iterate[i][j] = iterate[j][i] = system[i][j] / norm_scale
    root = None
    for sweep in range(NS_ITERS):
        prod = iterate if root is None else sym_product(root, iterate)
        update = [[None] * size for _ in range(size)]
        for i in range(size):
            for j in range(i, size):
                v = -0.5 * prod[i][j]
                update[i][j] = update[j][i] = 1.5 + v if i == j else v
        if sweep < NS_ITERS - 1:
            iterate = sym_product(iterate, update)
        root = update if root is None else sym_product(update, root)
    scale = jnp.sqrt((size - 1.0) / norm_scale)
    return [[root[k][i] * scale + mean_weight[k] for i in range(size)] for k in range(size)]


def kernel(
    sizes, x_ref, d_ref, wind_ref, obs_ref, var_ref, site_ref, count_ref, out,
    wind, count, obs, var, site,
    field, inside, made, ground, result, up_send, down_send, up_recv, down_recv,
    cols_send, cols_recv, load_sem, halo_send, halo_recv, ens_send, ens_recv, back_send, back_recv, own_sem,
):
    groups, subs, levels, high, wide, band, patches = sizes
    me, mine, core = lax.axis_index("grp"), lax.axis_index("sub"), lax.axis_index("rep")
    other = 1 - core
    tall, across = high + 2 * EDGE, wide + LANES
    has_up, has_down = mine > 0, mine < subs - 1
    loads = [
        pltpu.make_async_copy(x_ref, field.at[pl.ds(0, levels), pl.ds(EDGE, high), pl.ds(0, wide)], load_sem.at[0]),
        pltpu.make_async_copy(d_ref, field.at[levels, pl.ds(EDGE, high), pl.ds(0, wide)], load_sem.at[1]),
        pltpu.make_async_copy(wind_ref, wind, load_sem.at[2]),
    ]
    late_loads = [
        pltpu.make_async_copy(obs_ref, obs, load_sem.at[3]),
        pltpu.make_async_copy(var_ref, var, load_sem.at[4]),
        pltpu.make_async_copy(site_ref, site, load_sem.at[5]),
        pltpu.make_async_copy(count_ref, count, load_sem.at[6]),
    ]
    for c in loads + late_loads:
        c.start()

    barrier = pltpu.get_barrier_semaphore()
    for step in range(1, groups):
        peer = lax.rem(me + step, groups)
        pl.semaphore_signal(barrier, inc=1, device_id={"grp": peer}, device_id_type=MESH)
    pl.semaphore_signal(barrier, inc=1, device_id={"rep": other}, device_id_type=MESH)

    @pl.when(has_up)
    def _():
        pl.semaphore_signal(barrier, inc=1, device_id={"sub": mine - 1}, device_id_type=MESH)
        pl.semaphore_signal(barrier, inc=1, device_id={"sub": mine - 1, "rep": other}, device_id_type=MESH)

    @pl.when(has_down)
    def _():
        pl.semaphore_signal(barrier, inc=1, device_id={"sub": mine + 1}, device_id_type=MESH)
        pl.semaphore_signal(barrier, inc=1, device_id={"sub": mine + 1, "rep": other}, device_id_type=MESH)

    row = lax.broadcasted_iota(jnp.int32, (tall, across), 0) - EDGE
    col = lax.broadcasted_iota(jnp.int32, (tall, across), 1)
    row_ok = ((row >= 0) | has_up) & ((row < high) | has_down)
    row_ok = row_ok & (row >= -STEPS) & (row < high + STEPS)
    col_ok = (col < wide) | ((col < wide + STEPS) & (core == 0)) | ((col >= across - STEPS) & (core > 0))
    inside[...] = jnp.where(row_ok & col_ok, 1.0, 0.0)

    field[:, :, wide:across] = jnp.zeros((levels + 1, tall, LANES), jnp.float32)
    for c in loads:
        c.wait()

    fields = levels + 1
    lane = lax.broadcasted_iota(jnp.int32, (high, LANES), 1)
    slot_of_lane = lax.rem(lane + STEPS, LANES) // (2 * STEPS)
    packed = jnp.zeros((high, LANES), jnp.float32)
    for f in range(fields):
        inner = field[f, EDGE : EDGE + high, wide - LANES : wide]
        outer = field[f, EDGE : EDGE + high, 0:LANES]
        tile = jnp.where(core == 0, inner, outer)
        if f:
            tile = pltpu.roll(tile, 2 * STEPS * f, 1)
        packed = jnp.where(slot_of_lane == f, tile, packed)
    cols_send[...] = packed
    sub_row = lax.broadcasted_iota(jnp.int32, (EDGE, wide), 0)
    for k in range((fields + 1) // 2):
        a, b = 2 * k, min(2 * k + 1, fields - 1)
        top_a, top_b = field[a, EDGE : 2 * EDGE, 0:wide], field[b, EDGE : 2 * EDGE, 0:wide]
        low_a, low_b = field[a, high : high + EDGE, 0:wide], field[b, high : high + EDGE, 0:wide]
        up_send[k] = jnp.where(sub_row < STEPS, top_a, pltpu.roll(top_b, STEPS, 0))
        down_send[k] = jnp.where(sub_row >= STEPS, low_a, pltpu.roll(low_b, STEPS, 0))

    pl.semaphore_wait(
        barrier, groups + 2 * has_up.astype(jnp.int32) + 2 * has_down.astype(jnp.int32)
    )

    def halo(src, dst, n, device):
        return pltpu.make_async_remote_copy(
            src_ref=src, dst_ref=dst, send_sem=halo_send.at[n], recv_sem=halo_recv.at[n],
            device_id=device, device_id_type=MESH,
        )

    beside = halo(cols_send, cols_recv.at[pl.ds(EDGE, high)], 0, {"rep": other})
    beside.start()
    upward = [
        halo(up_send, down_recv, 1, {"sub": mine - 1}),
        halo(cols_send.at[pl.ds(0, EDGE)], cols_recv.at[pl.ds(EDGE + high, EDGE)], 2, {"sub": mine - 1, "rep": other}),
    ]
    downward = [
        halo(down_send, up_recv, 3, {"sub": mine + 1}),
        halo(cols_send.at[pl.ds(high - EDGE, EDGE)], cols_recv.at[pl.ds(0, EDGE)], 4, {"sub": mine + 1, "rep": other}),
    ]

    @pl.when(has_up)
    def _():
        for c in upward:
            c.start()

    @pl.when(has_down)
    def _():
        for c in downward:
            c.start()

    def place_columns(first, rows):
        got = cols_recv[first : first + rows]
        ok = inside[first : first + rows, wide:across] > 0.0
        for f in range(fields):
            tile = pltpu.roll(got, LANES - 2 * STEPS * f, 1) if f else got
            field[f, first : first + rows, wide:across] = jnp.where(ok, tile, 0.0)

    def forecast(level, first, rows):
        q = field[level, first : first + rows]
        d = field[levels, first : first + rows]
        wind_here = inside[first : first + rows] * wind[0, level]
        for _ in range(STEPS):
            west = pltpu.roll(q, 1, 1)
            east = pltpu.roll(q, across - 1, 1)
            north = pltpu.roll(q, 1, 0)
            south = pltpu.roll(q, rows - 1, 0)
            spread = (north + south) + (west + east) - 4.0 * q
            q = q + d * spread - wind_here * (q - west)
        return q[EDGE : rows - EDGE, 0:wide]

    def ensemble(level, target, owner, cells):
        return pltpu.make_async_remote_copy(
            src_ref=made.at[level, pl.ds(target * band, band), cells],
            dst_ref=ground.at[owner, level, :, cells],
            send_sem=ens_send.at[target], recv_sem=ens_recv.at[owner],
            device_id={"grp": target}, device_id_type=MESH,
        )

    def send_band(level, target, cells):
        @pl.when(me != target)
        def _():
            ensemble(level, target, me, cells).start()

    def middle(cells, left, right, level, carry):
        new = forecast(level, band, high - 2 * band + 2 * EDGE)
        made[level, band : high - band, cells] = jnp.where(core == 0, new[:, left], new[:, right])
        for target in range(1, groups - 1):
            send_band(level, target, cells)
        return carry

    far = pl.ds(pl.multiple_of(core * LANES, LANES), wide - LANES)
    near = pl.ds(pl.multiple_of((1 - core) * (wide - LANES), LANES), LANES)
    lax.fori_loop(
        0, levels, functools.partial(middle, far, slice(0, wide - LANES), slice(LANES, wide)), 0
    )
    beside.wait_recv()
    place_columns(EDGE, high)
    lax.fori_loop(
        0, levels, functools.partial(middle, near, slice(wide - LANES, wide), slice(0, LANES)), 0
    )

    @pl.when(has_up)
    def _():
        for c in downward:
            c.wait_recv()

    @pl.when(has_down)
    def _():
        for c in upward:
            c.wait_recv()

    place_columns(0, EDGE)
    place_columns(EDGE + high, EDGE)
    for f in range(fields):
        above, below = up_recv[f // 2], down_recv[f // 2]
        if f % 2:
            above, below = pltpu.roll(above, STEPS, 0), pltpu.roll(below, STEPS, 0)
        field[f, 0:EDGE, 0:wide] = jnp.where(inside[0:EDGE, 0:wide] > 0.0, above, 0.0)
        field[f, EDGE + high : tall, 0:wide] = jnp.where(inside[EDGE + high : tall, 0:wide] > 0.0, below, 0.0)

    def outer_bands(level, carry):
        made[level, 0:band] = forecast(level, 0, band + 2 * EDGE)
        send_band(level, 0, pl.ds(0, wide))
        made[level, high - band : high] = forecast(level, high - band, band + 2 * EDGE)
        send_band(level, groups - 1, pl.ds(0, wide))
        return carry

    lax.fori_loop(0, levels, outer_bands, 0)
    ground[me] = made[:, pl.ds(pl.multiple_of(me * band, band), band), :]

    def whole_band(target, owner):
        return pltpu.make_async_remote_copy(
            src_ref=made.at[:, pl.ds(target * band, band)],
            dst_ref=ground.at[owner],
            send_sem=ens_send.at[target], recv_sem=ens_recv.at[owner],
            device_id={"grp": target}, device_id_type=MESH,
        )

    for step in range(1, groups):
        peer = lax.rem(me + step, groups)
        whole_band(peer, peer).wait_recv()

    for c in late_loads:
        c.wait()
    patch = wide // patches
    tiles = [(h, p) for h in range(band // EDGE) for p in range(patches)]
    shape = (EDGE, LANES)
    lanes = lax.broadcasted_iota(jnp.int32, shape, 1)
    sub_lines = lax.broadcasted_iota(jnp.int32, shape, 0)
    system = [[None] * groups for _ in range(groups)]
    source = [None] * groups

    def put(old, new, index):
        new = jnp.broadcast_to(new, shape)
        return new if old is None else jnp.where(lanes == index, new, old)

    for index, (h, p) in enumerate(tiles):
        rows = slice(h * EDGE, (h + 1) * EDGE)
        here = site[rows, p, :]
        level_of, col_of = here // patch, lax.rem(here, patch)
        sampled = []
        for m in range(groups):
            got = jnp.zeros(shape, jnp.float32)
            for l in range(levels):
                tile = ground[m, l, rows, p * patch : (p + 1) * patch]
                pick = jnp.take_along_axis(tile, col_of, axis=1, mode="promise_in_bounds")
                got = jnp.where(level_of == l, pick, got)
            sampled.append(got)
        mean = sum(sampled[1:], sampled[0]) * (1.0 / groups)
        pert = [s - mean for s in sampled]
        live = jnp.zeros(shape, jnp.int32)
        for r in range(EDGE):
            live = jnp.where(sub_lines == r, count[p, h * EDGE + r], live)
        precision = jnp.where(lanes < live, 1.0 / var[rows, p, :], 0.0)
        innovation = obs[rows, p, :] - mean
        for i in range(groups):
            weighted = pert[i] * precision
            source[i] = put(source[i], jnp.sum(weighted * innovation, axis=1, keepdims=True), index)
            for j in range(i, groups):
                v = jnp.sum(weighted * pert[j], axis=1, keepdims=True)
                v = v + (groups - 1.0) if i == j else v
                system[i][j] = system[j][i] = put(system[i][j], v, index)
    combined = weights(system, source)

    def back(h, target, owner):
        return pltpu.make_async_remote_copy(
            src_ref=result.at[target, :, pl.ds(h * EDGE, EDGE)],
            dst_ref=out.at[:, pl.ds(owner * band + h * EDGE, EDGE)],
            send_sem=back_send.at[target], recv_sem=back_recv.at[owner],
            device_id={"grp": target}, device_id_type=MESH,
        )

    for h in range(band // EDGE):
        rows = slice(h * EDGE, (h + 1) * EDGE)
        for p in range(patches):
            index = h * patches + p
            c = [
                [jnp.broadcast_to(combined[k][i][:, index : index + 1], shape) for i in range(groups)]
                for k in range(groups)
            ]
            cells = slice(p * patch, (p + 1) * patch)
            for l in range(levels):
                member = [ground[m, l, rows, cells] for m in range(groups)]
                mean = sum(member[1:], member[0]) * (1.0 / groups)
                pert = [v - mean for v in member]
                for i in range(groups):
                    v = c[0][i] * pert[0]
                    for k in range(1, groups):
                        v = v + c[k][i] * pert[k]
                    result[i, l, rows, cells] = mean + v
        for step in range(1, groups):
            peer = lax.rem(me + step, groups)
            back(h, peer, me).start()
    own = pltpu.make_async_copy(result.at[me], out.at[:, pl.ds(me * band, band)], own_sem)
    own.start()

    beside.wait_send()

    @pl.when(has_up)
    def _():
        for c in upward:
            c.wait_send()

    @pl.when(has_down)
    def _():
        for c in downward:
            c.wait_send()

    def whole_back(target, owner):
        return pltpu.make_async_remote_copy(
            src_ref=result.at[target],
            dst_ref=out.at[:, pl.ds(owner * band, band)],
            send_sem=back_send.at[target], recv_sem=back_recv.at[owner],
            device_id={"grp": target}, device_id_type=MESH,
        )

    for step in range(1, groups):
        peer = lax.rem(me + step, groups)
        whole_band(peer, me).wait_send()
        whole_back(peer, me).wait_send()
        whole_back(peer, peer).wait_recv()
    own.wait()


def fused(state, diffusivity, wind, observed, variance, site, count):
    groups, subs = lax.axis_size("grp"), lax.axis_size("sub")
    _, levels, high, wide = state.shape
    band, patches, _ = observed.shape
    tall, across = high + 2 * EDGE, wide + LANES
    pairs = (levels + 2) // 2
    f32 = jnp.float32
    vmem, dma = pltpu.VMEM, pltpu.SemaphoreType.DMA
    in_hbm = pl.BlockSpec(memory_space=pltpu.HBM)
    anywhere = pl.BlockSpec(memory_space=pl.ANY)
    sizes = (groups, subs, levels, high, wide, band, patches)
    out = pl.pallas_call(
        functools.partial(kernel, sizes),
        out_shape=jax.ShapeDtypeStruct((levels, high, wide), f32),
        in_specs=[in_hbm] * 7,
        out_specs=anywhere,
        scratch_shapes=[
            pltpu.SMEM(wind.shape, f32),
            pltpu.SMEM(count.shape[::-1], jnp.int32),
            vmem(observed.shape, f32),
            vmem(observed.shape, f32),
            vmem(observed.shape, jnp.int32),
            vmem((levels + 1, tall, across), f32),
            vmem((tall, across), f32),
            vmem((levels, high, wide), f32),
            vmem((groups, levels, band, wide), f32),
            vmem((groups, levels, band, wide), f32),
            vmem((pairs, EDGE, wide), f32),
            vmem((pairs, EDGE, wide), f32),
            vmem((pairs, EDGE, wide), f32),
            vmem((pairs, EDGE, wide), f32),
            vmem((high, LANES), f32),
            vmem((tall, LANES), f32),
            dma((7,)),
            dma((5,)),
            dma((5,)),
            dma((groups,)),
            dma((groups,)),
            dma((groups,)),
            dma((groups,)),
            dma(()),
        ],
        compiler_params=pltpu.CompilerParams(collective_id=0, has_side_effects=True, vmem_limit_bytes=SCOPED),
    )(*[
        pltpu.with_memory_space_constraint(v, pltpu.HBM)
        for v in (state[0], diffusivity, wind, observed, variance, site, count.T)
    ])
    return out[None]


def on_device(
    starting_concentration_per_run,
    diffusivity,
    run_layer_stability_number,
    observed,
    slot_error_variance,
    sensor_target_site,
    patch_live_count,
):
    groups, subs, reps = lax.axis_size("grp"), lax.axis_size("sub"), lax.axis_size("rep")
    members, levels, high, wide = starting_concentration_per_run.shape
    band, patches, slots = observed.shape
    fits = (
        members == 1
        and reps == 2
        and 3 <= groups <= 8
        and subs >= 2
        and band % EDGE == 0
        and 2 * STEPS * (levels + 1) <= LANES
        and wide == patches * PATCH
        and PATCH == LANES == slots
    )
    step = fused if fits else on_device_plain
    return step(
        starting_concentration_per_run,
        diffusivity,
        run_layer_stability_number,
        observed,
        slot_error_variance,
        sensor_target_site,
        patch_live_count,
    )


def solution(mesh):
    in_specs = (
        P("grp", None, "sub", "rep"),
        P("sub", "rep"),
        P("grp", None),
        P(("sub", "grp"), "rep", None),
        P(("sub", "grp"), "rep", None),
        P(("sub", "grp"), "rep", None),
        P(("sub", "grp"), "rep"),
    )
    out_specs = P("grp", None, "sub", "rep")
    return jax.shard_map(
        on_device, mesh=mesh, in_specs=in_specs, out_specs=out_specs, check_vma=False
    )
```

```python
import functools

import jax
import jax.numpy as jnp
from jax import lax
from jax.experimental import pallas as pl
from jax.experimental.pallas import tpu as pltpu
from jax.sharding import PartitionSpec as P

PATCH = 128
STEPS = 4
NS_ITERS = 4


HIGHEST = lax.Precision.HIGHEST


def extended(x, sides, width):
    for axis, dim in sides:
        devices, length = (lax.axis_size(axis), x.shape[dim])
        up = [(i, (i + 1) % devices) for i in range(devices - 1)]
        down = [(j, i) for i, j in up]
        last = lax.slice_in_dim(x, length - width, length, axis=dim)
        initial = lax.slice_in_dim(x, 0, width, axis=dim)
        before = lax.ppermute(last, axis, up)
        after = lax.ppermute(initial, axis, down)
        x = jnp.concatenate([before, x, after], axis=dim)
    return x


def advance(padded, diffusivity, member_wind):
    centre = padded[..., 1:-1, 1:-1]
    northern = padded[..., :-2, 1:-1]
    southern = padded[..., 2:, 1:-1]
    western = padded[..., 1:-1, :-2]
    easterly_side = padded[..., 1:-1, 2:]
    spread = northern + southern + (western + easterly_side) - 4.0 * centre
    return centre + diffusivity * spread - member_wind * (centre - western)


def analyse(background, sampled, observed, slot_error_variance, patch_live_count):
    members = background.shape[1]
    slots = observed.shape[-1]
    centre_mean = jnp.mean(background, axis=1, keepdims=True)
    perturbed = background - centre_mean
    sampled_mean = jnp.mean(sampled, axis=1, keepdims=True)
    sampled_pert = sampled - sampled_mean
    live_slot = jnp.arange(slots)[None, :] < patch_live_count[:, None]
    precision_obs = jnp.where(live_slot, 1.0 / slot_error_variance, 0.0 * slot_error_variance)
    innovation = observed - sampled_mean[:, 0, :]
    weighted = sampled_pert * precision_obs[:, None, :]
    identity = jnp.eye(members, dtype=background.dtype)
    system = (
        jnp.einsum("pms,pns->pmn", weighted, sampled_pert, precision=HIGHEST)
        + (members - 1.0) * identity
    )
    source_term = jnp.einsum("pms,ps->pm", weighted, innovation, precision=HIGHEST)
    factor = jnp.linalg.cholesky(system)
    halfway = lax.linalg.triangular_solve(
        factor, source_term[:, :, None], left_side=True, lower=True
    )
    mean_weight = lax.linalg.triangular_solve(
        factor, halfway, left_side=True, lower=True, transpose_a=True
    )[:, :, 0]
    norm_scale = jnp.sqrt(jnp.sum(system * system, axis=(1, 2)))
    iterate = system / norm_scale[:, None, None]
    inverse_root = jnp.broadcast_to(identity, system.shape)
    for sweep in range(NS_ITERS):
        update = 1.5 * identity - 0.5 * jnp.einsum(
            "pij,pjk->pik", inverse_root, iterate, precision=HIGHEST
        )
        iterate = jnp.einsum("pij,pjk->pik", iterate, update, precision=HIGHEST)
        inverse_root = jnp.einsum("pij,pjk->pik", update, inverse_root, precision=HIGHEST)
    spread_weight = inverse_root * jnp.sqrt((members - 1.0) / norm_scale)[:, None, None]
    combined = spread_weight + mean_weight[:, :, None]
    return centre_mean + jnp.einsum("pki,pkc->pic", combined, perturbed, precision=HIGHEST)


def on_device_plain(
    starting_concentration_per_run,
    diffusivity,
    run_layer_stability_number,
    observed,
    slot_error_variance,
    sensor_target_site,
    patch_live_count,
):
    member_wind = run_layer_stability_number[:, :, None, None]
    present_state = starting_concentration_per_run
    for stepno in range(STEPS):
        padded = extended(present_state, (("sub", 2), ("rep", 3)), 1)
        present_state = advance(padded, diffusivity, member_wind)
    gathered = lax.all_to_all(present_state, "grp", split_axis=2, concat_axis=0, tiled=True)
    members, levels, row_group, row_width = gathered.shape
    patches = row_width // PATCH
    background = jnp.transpose(
        gathered.reshape(members, levels, row_group, patches, PATCH), (2, 3, 0, 1, 4)
    ).reshape(row_group * patches, members, levels * PATCH)
    slots = observed.shape[-1]
    cell_flat = sensor_target_site.reshape(-1, slots)
    selector = (cell_flat[:, :, None] == jnp.arange(levels * PATCH)[None, None, :]).astype(
        jnp.float32
    )
    sampled = jnp.einsum("pmc,psc->pms", background, selector, precision=HIGHEST)
    result = analyse(
        background,
        sampled,
        observed.reshape(-1, slots),
        slot_error_variance.reshape(-1, slots),
        patch_live_count.reshape(-1),
    )
    returned = jnp.transpose(
        result.reshape(row_group, patches, members, levels, PATCH), (2, 3, 0, 1, 4)
    ).reshape(members, levels, row_group, row_width)
    return lax.all_to_all(returned, "grp", split_axis=0, concat_axis=2, tiled=True)


EDGE = 8
SCOPED = 24 * 1024 * 1024
LANES = 128
MESH = pl.DeviceIdType.MESH


def sym_product(a, b):
    size = len(a)
    c = [[None] * size for _ in range(size)]
    for i in range(size):
        for j in range(i, size):
            total = a[i][0] * b[0][j]
            for k in range(1, size):
                total = total + a[i][k] * b[k][j]
            c[i][j] = c[j][i] = total
    return c


def weights(system, source):
    size = len(system)
    low = [[None] * size for _ in range(size)]
    for j in range(size):
        diag = system[j][j]
        for k in range(j):
            diag = diag - low[j][k] * low[j][k]
        low[j][j] = jnp.sqrt(diag)
        for i in range(j + 1, size):
            v = system[i][j]
            for k in range(j):
                v = v - low[i][k] * low[j][k]
            low[i][j] = v / low[j][j]
    half = []
    for i in range(size):
        v = source[i]
        for k in range(i):
            v = v - low[i][k] * half[k]
        half.append(v / low[i][i])
    mean_weight = [None] * size
    for i in reversed(range(size)):
        v = half[i]
        for k in range(i + 1, size):
            v = v - low[k][i] * mean_weight[k]
        mean_weight[i] = v / low[i][i]
    total = None
    for i in range(size):
        for j in range(size):
            sq = system[i][j] * system[i][j]
            total = sq if total is None else total + sq
    norm_scale = jnp.sqrt(total)
    iterate = [[None] * size for _ in range(size)]
    for i in range(size):
        for j in range(i, size):
            iterate[i][j] = iterate[j][i] = system[i][j] / norm_scale
    root = None
    for sweep in range(NS_ITERS):
        prod = iterate if root is None else sym_product(root, iterate)
        update = [[None] * size for _ in range(size)]
        for i in range(size):
            for j in range(i, size):
                v = -0.5 * prod[i][j]
                update[i][j] = update[j][i] = 1.5 + v if i == j else v
        if sweep < NS_ITERS - 1:
            iterate = sym_product(iterate, update)
        root = update if root is None else sym_product(update, root)
    scale = jnp.sqrt((size - 1.0) / norm_scale)
    return [[root[k][i] * scale + mean_weight[k] for i in range(size)] for k in range(size)]


def kernel(
    sizes, x_ref, d_ref, wind_ref, obs_ref, var_ref, site_ref, count_ref, out,
    wind, count, obs, var, site,
    field, inside, made, ground, result, up_send, down_send, up_recv, down_recv,
    cols_send, cols_recv, load_sem, halo_send, halo_recv, ens_send, ens_recv, back_send, back_recv, own_sem,
):
    groups, subs, levels, high, wide, band, patches = sizes
    me, mine, core = lax.axis_index("grp"), lax.axis_index("sub"), lax.axis_index("rep")
    other = 1 - core
    tall, across = high + 2 * EDGE, wide + LANES
    has_up, has_down = mine > 0, mine < subs - 1
    loads = [
        pltpu.make_async_copy(x_ref, field.at[pl.ds(0, levels), pl.ds(EDGE, high), pl.ds(0, wide)], load_sem.at[0]),
        pltpu.make_async_copy(d_ref, field.at[levels, pl.ds(EDGE, high), pl.ds(0, wide)], load_sem.at[1]),
        pltpu.make_async_copy(wind_ref, wind, load_sem.at[2]),
    ]
    late_loads = [
        pltpu.make_async_copy(obs_ref, obs, load_sem.at[3]),
        pltpu.make_async_copy(var_ref, var, load_sem.at[4]),
        pltpu.make_async_copy(site_ref, site, load_sem.at[5]),
        pltpu.make_async_copy(count_ref, count, load_sem.at[6]),
    ]
    for c in loads + late_loads:
        c.start()

    barrier = pltpu.get_barrier_semaphore()
    for step in range(1, groups):
        peer = lax.rem(me + step, groups)
        pl.semaphore_signal(barrier, inc=1, device_id={"grp": peer}, device_id_type=MESH)
    pl.semaphore_signal(barrier, inc=1, device_id={"rep": other}, device_id_type=MESH)

    @pl.when(has_up)
    def _():
        pl.semaphore_signal(barrier, inc=1, device_id={"sub": mine - 1}, device_id_type=MESH)
        pl.semaphore_signal(barrier, inc=1, device_id={"sub": mine - 1, "rep": other}, device_id_type=MESH)

    @pl.when(has_down)
    def _():
        pl.semaphore_signal(barrier, inc=1, device_id={"sub": mine + 1}, device_id_type=MESH)
        pl.semaphore_signal(barrier, inc=1, device_id={"sub": mine + 1, "rep": other}, device_id_type=MESH)

    row = lax.broadcasted_iota(jnp.int32, (tall, across), 0) - EDGE
    col = lax.broadcasted_iota(jnp.int32, (tall, across), 1)
    row_ok = ((row >= 0) | has_up) & ((row < high) | has_down)
    row_ok = row_ok & (row >= -STEPS) & (row < high + STEPS)
    col_ok = (col < wide) | ((col < wide + STEPS) & (core == 0)) | ((col >= across - STEPS) & (core > 0))
    inside[...] = jnp.where(row_ok & col_ok, 1.0, 0.0)

    field[:, :, wide:across] = jnp.zeros((levels + 1, tall, LANES), jnp.float32)
    for c in loads:
        c.wait()

    fields = levels + 1
    lane = lax.broadcasted_iota(jnp.int32, (high, LANES), 1)
    slot_of_lane = lax.rem(lane + STEPS, LANES) // (2 * STEPS)
    packed = jnp.zeros((high, LANES), jnp.float32)
    for f in range(fields):
        inner = field[f, EDGE : EDGE + high, wide - LANES : wide]
        outer = field[f, EDGE : EDGE + high, 0:LANES]
        tile = jnp.where(core == 0, inner, outer)
        if f:
            tile = pltpu.roll(tile, 2 * STEPS * f, 1)
        packed = jnp.where(slot_of_lane == f, tile, packed)
    cols_send[...] = packed
    sub_row = lax.broadcasted_iota(jnp.int32, (EDGE, wide), 0)
    for k in range((fields + 1) // 2):
        a, b = 2 * k, min(2 * k + 1, fields - 1)
        top_a, top_b = field[a, EDGE : 2 * EDGE, 0:wide], field[b, EDGE : 2 * EDGE, 0:wide]
        low_a, low_b = field[a, high : high + EDGE, 0:wide], field[b, high : high + EDGE, 0:wide]
        up_send[k] = jnp.where(sub_row < STEPS, top_a, pltpu.roll(top_b, STEPS, 0))
        down_send[k] = jnp.where(sub_row >= STEPS, low_a, pltpu.roll(low_b, STEPS, 0))

    pl.semaphore_wait(
        barrier, groups + 2 * has_up.astype(jnp.int32) + 2 * has_down.astype(jnp.int32)
    )

    def halo(src, dst, n, device):
        return pltpu.make_async_remote_copy(
            src_ref=src, dst_ref=dst, send_sem=halo_send.at[n], recv_sem=halo_recv.at[n],
            device_id=device, device_id_type=MESH,
        )

    beside = halo(cols_send, cols_recv.at[pl.ds(EDGE, high)], 0, {"rep": other})
    beside.start()
    upward = [
        halo(up_send, down_recv, 1, {"sub": mine - 1}),
        halo(cols_send.at[pl.ds(0, EDGE)], cols_recv.at[pl.ds(EDGE + high, EDGE)], 2, {"sub": mine - 1, "rep": other}),
    ]
    downward = [
        halo(down_send, up_recv, 3, {"sub": mine + 1}),
        halo(cols_send.at[pl.ds(high - EDGE, EDGE)], cols_recv.at[pl.ds(0, EDGE)], 4, {"sub": mine + 1, "rep": other}),
    ]

    @pl.when(has_up)
    def _():
        for c in upward:
            c.start()

    @pl.when(has_down)
    def _():
        for c in downward:
            c.start()

    def place_columns(first, rows):
        got = cols_recv[first : first + rows]
        ok = inside[first : first + rows, wide:across] > 0.0
        for f in range(fields):
            tile = pltpu.roll(got, LANES - 2 * STEPS * f, 1) if f else got
            field[f, first : first + rows, wide:across] = jnp.where(ok, tile, 0.0)

    def forecast(level, first, rows):
        q = field[level, first : first + rows]
        d = field[levels, first : first + rows]
        wind_here = inside[first : first + rows] * wind[0, level]
        for _ in range(STEPS):
            west = pltpu.roll(q, 1, 1)
            east = pltpu.roll(q, across - 1, 1)
            north = pltpu.roll(q, 1, 0)
            south = pltpu.roll(q, rows - 1, 0)
            spread = (north + south) + (west + east) - 4.0 * q
            q = q + d * spread - wind_here * (q - west)
        return q[EDGE : rows - EDGE, 0:wide]

    def ensemble(level, target, owner, first, rows, cells):
        return pltpu.make_async_remote_copy(
            src_ref=made.at[level, pl.ds(target * band + first, rows), cells],
            dst_ref=ground.at[owner, level, pl.ds(first, rows), cells],
            send_sem=ens_send.at[target], recv_sem=ens_recv.at[owner],
            device_id={"grp": target}, device_id_type=MESH,
        )

    def send_band(level, target, first, rows, cells):
        @pl.when(me != target)
        def _():
            ensemble(level, target, me, first, rows, cells).start()

    def middle(cells, left, right, level, carry):
        new = forecast(level, EDGE, high)
        made[level, EDGE : high - EDGE, cells] = jnp.where(core == 0, new[:, left], new[:, right])
        send_band(level, 0, EDGE, band - EDGE, cells)
        send_band(level, groups - 1, 0, band - EDGE, cells)
        for target in range(1, groups - 1):
            send_band(level, target, 0, band, cells)
        return carry

    far = pl.ds(pl.multiple_of(core * LANES, LANES), wide - LANES)
    near = pl.ds(pl.multiple_of((1 - core) * (wide - LANES), LANES), LANES)
    lax.fori_loop(
        0, levels, functools.partial(middle, far, slice(0, wide - LANES), slice(LANES, wide)), 0
    )
    beside.wait_recv()
    place_columns(EDGE, high)
    lax.fori_loop(
        0, levels, functools.partial(middle, near, slice(wide - LANES, wide), slice(0, LANES)), 0
    )

    @pl.when(has_up)
    def _():
        for c in downward:
            c.wait_recv()

    @pl.when(has_down)
    def _():
        for c in upward:
            c.wait_recv()

    place_columns(0, EDGE)
    place_columns(EDGE + high, EDGE)
    for f in range(fields):
        above, below = up_recv[f // 2], down_recv[f // 2]
        if f % 2:
            above, below = pltpu.roll(above, STEPS, 0), pltpu.roll(below, STEPS, 0)
        field[f, 0:EDGE, 0:wide] = jnp.where(inside[0:EDGE, 0:wide] > 0.0, above, 0.0)
        field[f, EDGE + high : tall, 0:wide] = jnp.where(inside[EDGE + high : tall, 0:wide] > 0.0, below, 0.0)

    def outer_bands(level, carry):
        made[level, 0:EDGE] = forecast(level, 0, 3 * EDGE)
        send_band(level, 0, 0, EDGE, pl.ds(0, wide))
        made[level, high - EDGE : high] = forecast(level, high - EDGE, 3 * EDGE)
        send_band(level, groups - 1, band - EDGE, EDGE, pl.ds(0, wide))
        return carry

    lax.fori_loop(0, levels, outer_bands, 0)
    ground[me] = made[:, pl.ds(pl.multiple_of(me * band, band), band), :]

    def whole_band(target, owner):
        return pltpu.make_async_remote_copy(
            src_ref=made.at[:, pl.ds(target * band, band)],
            dst_ref=ground.at[owner],
            send_sem=ens_send.at[target], recv_sem=ens_recv.at[owner],
            device_id={"grp": target}, device_id_type=MESH,
        )

    for step in range(1, groups):
        peer = lax.rem(me + step, groups)
        whole_band(peer, peer).wait_recv()

    for c in late_loads:
        c.wait()
    patch = wide // patches
    tiles = [(h, p) for h in range(band // EDGE) for p in range(patches)]
    shape = (EDGE, LANES)
    lanes = lax.broadcasted_iota(jnp.int32, shape, 1)
    sub_lines = lax.broadcasted_iota(jnp.int32, shape, 0)
    system = [[None] * groups for _ in range(groups)]
    source = [None] * groups

    def put(old, new, index):
        new = jnp.broadcast_to(new, shape)
        return new if old is None else jnp.where(lanes == index, new, old)

    for index, (h, p) in enumerate(tiles):
        rows = slice(h * EDGE, (h + 1) * EDGE)
        here = site[rows, p, :]
        level_of, col_of = here // patch, lax.rem(here, patch)
        sampled = []
        for m in range(groups):
            got = jnp.zeros(shape, jnp.float32)
            for l in range(levels):
                tile = ground[m, l, rows, p * patch : (p + 1) * patch]
                pick = jnp.take_along_axis(tile, col_of, axis=1, mode="promise_in_bounds")
                got = jnp.where(level_of == l, pick, got)
            sampled.append(got)
        mean = sum(sampled[1:], sampled[0]) * (1.0 / groups)
        pert = [s - mean for s in sampled]
        live = jnp.zeros(shape, jnp.int32)
        for r in range(EDGE):
            live = jnp.where(sub_lines == r, count[p, h * EDGE + r], live)
        precision = jnp.where(lanes < live, 1.0 / var[rows, p, :], 0.0)
        innovation = obs[rows, p, :] - mean
        for i in range(groups):
            weighted = pert[i] * precision
            source[i] = put(source[i], jnp.sum(weighted * innovation, axis=1, keepdims=True), index)
            for j in range(i, groups):
                v = jnp.sum(weighted * pert[j], axis=1, keepdims=True)
                v = v + (groups - 1.0) if i == j else v
                system[i][j] = system[j][i] = put(system[i][j], v, index)
    combined = weights(system, source)

    def back(h, target, owner):
        return pltpu.make_async_remote_copy(
            src_ref=result.at[target, :, pl.ds(h * EDGE, EDGE)],
            dst_ref=out.at[:, pl.ds(owner * band + h * EDGE, EDGE)],
            send_sem=back_send.at[target], recv_sem=back_recv.at[owner],
            device_id={"grp": target}, device_id_type=MESH,
        )

    for h in range(band // EDGE):
        rows = slice(h * EDGE, (h + 1) * EDGE)
        for p in range(patches):
            index = h * patches + p
            c = [
                [jnp.broadcast_to(combined[k][i][:, index : index + 1], shape) for i in range(groups)]
                for k in range(groups)
            ]
            cells = slice(p * patch, (p + 1) * patch)
            for l in range(levels):
                member = [ground[m, l, rows, cells] for m in range(groups)]
                mean = sum(member[1:], member[0]) * (1.0 / groups)
                pert = [v - mean for v in member]
                for i in range(groups):
                    v = c[0][i] * pert[0]
                    for k in range(1, groups):
                        v = v + c[k][i] * pert[k]
                    result[i, l, rows, cells] = mean + v
        for step in range(1, groups):
            peer = lax.rem(me + step, groups)
            back(h, peer, me).start()
    own = pltpu.make_async_copy(result.at[me], out.at[:, pl.ds(me * band, band)], own_sem)
    own.start()

    beside.wait_send()

    @pl.when(has_up)
    def _():
        for c in upward:
            c.wait_send()

    @pl.when(has_down)
    def _():
        for c in downward:
            c.wait_send()

    def whole_back(target, owner):
        return pltpu.make_async_remote_copy(
            src_ref=result.at[target],
            dst_ref=out.at[:, pl.ds(owner * band, band)],
            send_sem=back_send.at[target], recv_sem=back_recv.at[owner],
            device_id={"grp": target}, device_id_type=MESH,
        )

    for step in range(1, groups):
        peer = lax.rem(me + step, groups)
        whole_band(peer, me).wait_send()
        whole_back(peer, me).wait_send()
        whole_back(peer, peer).wait_recv()
    own.wait()


def fused(state, diffusivity, wind, observed, variance, site, count):
    groups, subs = lax.axis_size("grp"), lax.axis_size("sub")
    _, levels, high, wide = state.shape
    band, patches, _ = observed.shape
    tall, across = high + 2 * EDGE, wide + LANES
    pairs = (levels + 2) // 2
    f32 = jnp.float32
    vmem, dma = pltpu.VMEM, pltpu.SemaphoreType.DMA
    in_hbm = pl.BlockSpec(memory_space=pltpu.HBM)
    anywhere = pl.BlockSpec(memory_space=pl.ANY)
    sizes = (groups, subs, levels, high, wide, band, patches)
    out = pl.pallas_call(
        functools.partial(kernel, sizes),
        out_shape=jax.ShapeDtypeStruct((levels, high, wide), f32),
        in_specs=[in_hbm] * 7,
        out_specs=anywhere,
        scratch_shapes=[
            pltpu.SMEM(wind.shape, f32),
            pltpu.SMEM(count.shape[::-1], jnp.int32),
            vmem(observed.shape, f32),
            vmem(observed.shape, f32),
            vmem(observed.shape, jnp.int32),
            vmem((levels + 1, tall, across), f32),
            vmem((tall, across), f32),
            vmem((levels, high, wide), f32),
            vmem((groups, levels, band, wide), f32),
            vmem((groups, levels, band, wide), f32),
            vmem((pairs, EDGE, wide), f32),
            vmem((pairs, EDGE, wide), f32),
            vmem((pairs, EDGE, wide), f32),
            vmem((pairs, EDGE, wide), f32),
            vmem((high, LANES), f32),
            vmem((tall, LANES), f32),
            dma((7,)),
            dma((5,)),
            dma((5,)),
            dma((groups,)),
            dma((groups,)),
            dma((groups,)),
            dma((groups,)),
            dma(()),
        ],
        compiler_params=pltpu.CompilerParams(collective_id=0, has_side_effects=True, vmem_limit_bytes=SCOPED),
    )(*[
        pltpu.with_memory_space_constraint(v, pltpu.HBM)
        for v in (state[0], diffusivity, wind, observed, variance, site, count.T)
    ])
    return out[None]


def on_device(
    starting_concentration_per_run,
    diffusivity,
    run_layer_stability_number,
    observed,
    slot_error_variance,
    sensor_target_site,
    patch_live_count,
):
    groups, subs, reps = lax.axis_size("grp"), lax.axis_size("sub"), lax.axis_size("rep")
    members, levels, high, wide = starting_concentration_per_run.shape
    band, patches, slots = observed.shape
    fits = (
        members == 1
        and reps == 2
        and 3 <= groups <= 8
        and subs >= 2
        and band % EDGE == 0
        and band >= 2 * EDGE
        and 2 * STEPS * (levels + 1) <= LANES
        and wide == patches * PATCH
        and PATCH == LANES == slots
    )
    step = fused if fits else on_device_plain
    return step(
        starting_concentration_per_run,
        diffusivity,
        run_layer_stability_number,
        observed,
        slot_error_variance,
        sensor_target_site,
        patch_live_count,
    )


def solution(mesh):
    in_specs = (
        P("grp", None, "sub", "rep"),
        P("sub", "rep"),
        P("grp", None),
        P(("sub", "grp"), "rep", None),
        P(("sub", "grp"), "rep", None),
        P(("sub", "grp"), "rep", None),
        P(("sub", "grp"), "rep"),
    )
    out_specs = P("grp", None, "sub", "rep")
    return jax.shard_map(
        on_device, mesh=mesh, in_specs=in_specs, out_specs=out_specs, check_vma=False
    )
```
